256 devices in a mesh: vel: 4 (over y_hi, core), space: 64 (over z, x, y_lo).
Axes of the slice: x: 4, y: 4 (y_hi: 2, y_lo: 2; y = y_hi * 2 + y_lo), z: 8, core: 2. Of those that a mesh axis runs over, the one named last changes fastest.
Arguments:
- distribution: float32 [13824, 128, 128], P('vel', 'space'), may hold values from -4 to 4
- vel_index: int32 [13824], P('vel'), may hold values from 0 to 13823, as said below
- collision_time: float32 [128, 128], P('space'), may hold values from 0.5 to 4
- wall_flags: int32 [128, 128], P('space'), may hold values 0 or 1
- wall_temp: float32 [128, 128], P('space'), may hold values from -2 to 2
Outputs:
- distribution_new: float32 [13824, 128, 128], P('vel', 'space')
- correction: float32 [128, 128], P('space')
The draws below stay inside these ranges and needn't reach their ends.
Inputs may be any that keep to these rules, and one draw needn't show every extreme that they name: `vel_index`: a permutation of 0 to 13823; in each aligned block of 13824 // 4 slots exactly half of the values have index_x >= 12.
All inputs are finite; a program needn't handle non-finite values. No bound on the sum of `wall_flags` on one device may be relied on, other than what follows from the above.
Results may differ from the reference program's by a relative error of at most 0.0003.
Values sent between devices are 32-bit elements; how exact they have to be, the bound alone decides.
No kernel may reach another device: no remote copies, remote signals or barrier semaphores. Data moves between devices by JAX's collectives and lax.ppermute only.
A program may use at most 64 MiB of HBM per device.

```python
import math
import jax
import jax.numpy as jnp
from jax import lax

VGRID = 24
VEL = 13824
NY = 128
ITERS = 3
NX = 128
N_VEL = 4


def draw_vel_index(key, part):
    half_total = VEL // 2
    per_block = VEL // N_VEL
    half_block = per_block // 2
    key_low = jax.random.fold_in(key, 11)
    key_high = jax.random.fold_in(key, 23)
    key_mix = jax.random.fold_in(key, 37)
    lower = jax.random.permutation(key_low, half_total).astype(jnp.int32)
    higher = jax.random.permutation(key_high, half_total).astype(jnp.int32) + half_total
    grouped = jnp.concatenate([lower.reshape(N_VEL, half_block), higher.reshape(N_VEL, half_block)], axis=1)
    block_keys = jax.random.split(key_mix, N_VEL)
    mixing = jax.vmap(lambda one_key: jax.random.permutation(one_key, per_block).astype(jnp.int32))(block_keys)
    mixed = jnp.take_along_axis(grouped, mixing, axis=1)
    return mixed.reshape(VEL).astype(jnp.int32)


def set_ends(array, own_key, least, largest):
    longest = array.shape.index(max(array.shape))
    spots = []
    for shift in (0, 1):
        where = [jax.random.randint(jax.random.fold_in(own_key, axis), (), 0, length) for axis, length in enumerate(array.shape)]
        where[longest] = (where[longest] + shift) % array.shape[longest]
        spots.append(tuple(where))
    return array.at[spots[0]].set(least).at[spots[1]].set(largest)


def shard_levels(key, extent, cuts, least, largest):
    def one(axis_at, blocks):
        heights = jax.random.uniform(jax.random.fold_in(jax.random.fold_in(key, 6), axis_at), (blocks,), jnp.float32, least / len(cuts), largest / len(cuts))
        return jnp.repeat(jnp.exp(heights), extent[axis_at] // blocks).reshape((-1,) + (1,) * (len(extent) - axis_at - 1))

    loudness = one(*cuts[0])
    for cut in cuts[1:]:
        loudness = loudness * one(*cut)
    return loudness


def noise(own_key, extent, deviation, limit, cuts=(), held_as=jnp.bfloat16):
    drawn = jax.random.normal(own_key, extent, jnp.float32) * deviation
    if len(cuts) > 0:
        drawn = shard_levels(own_key, extent, cuts, -0.22, 0.18) * drawn
    return jnp.clip(drawn, min=-limit, max=limit).astype(held_as)


def setup_inputs(seed: int = 0) -> dict:
    key_of = jax.random.split(jax.random.key(seed), 6)
    distribution = noise(key_of[0], (VEL, NX, NY), 0.3, 4.0, ((0, 4), (1, 64)), jnp.float32)
    vel_index = draw_vel_index(jax.random.fold_in(key_of[5], 71), 0)
    collision_time = jnp.clip(jnp.exp(math.log(4.0) - 2.0794415 * jax.random.uniform(key_of[2], (NX, NY), jnp.float32) ** shard_levels(key_of[2], (NX, NY), ((0, 64),), -0.2, 0.2)), 0.5, 4.0)
    wall_flags = set_ends((jax.random.randint(key_of[3], (NX, NY), 0, 8) < 1).astype(jnp.int32), jax.random.fold_in(key_of[3], 1), 0, 1)
    wall_temp = jnp.clip(jax.random.uniform(key_of[4], (NX, NY), jnp.float32, -2.0, 2.0) * shard_levels(key_of[4], (NX, NY), ((0, 64),), -0.4, 0.0), -2.0, 2.0)
    return {"distribution": distribution, "vel_index": vel_index, "collision_time": collision_time, "wall_flags": wall_flags, "wall_temp": wall_temp}


VELOCITY_MAX = 4.5
COOLING = 0.08
SHAKHOV = 0.8 * (1.0 - 2.0 / 3.0)


def velocity_tables(slot_ids):
    index_x = slot_ids // (VGRID * VGRID)
    index_y = (slot_ids // VGRID) % VGRID
    index_z = slot_ids % VGRID
    spacing = 2.0 * VELOCITY_MAX / VGRID
    speed_x = -VELOCITY_MAX + (index_x.astype(jnp.float32) + 0.5) * spacing
    speed_y = -VELOCITY_MAX + (index_y.astype(jnp.float32) + 0.5) * spacing
    speed_z = -VELOCITY_MAX + (index_z.astype(jnp.float32) + 0.5) * spacing
    speed_sq = speed_x * speed_x + speed_y * speed_y + speed_z * speed_z
    weight = spacing ** 3
    unity = jnp.ones_like(speed_x)
    heat_x = speed_x * (speed_sq - 2.5)
    heat_y = speed_y * (speed_sq - 2.5)
    heat_z = speed_z * (speed_sq - 2.5)
    moment_rows = jnp.stack([unity, speed_x, speed_y, speed_z, (2.0 / 3.0) * speed_sq - 1.0, heat_x, heat_y, heat_z]) * weight
    maxwell = jnp.exp(-speed_sq) * math.pi ** -1.5
    temp_shape = (speed_sq - 1.5) * maxwell
    shape_rows = jnp.stack([maxwell, 2.0 * speed_x * maxwell, 2.0 * speed_y * maxwell, 2.0 * speed_z * maxwell,
                            (1.0 - COOLING) * temp_shape, SHAKHOV * heat_x * maxwell, SHAKHOV * heat_y * maxwell,
                            SHAKHOV * heat_z * maxwell])
    return speed_x, speed_y, moment_rows, shape_rows, temp_shape


def wall_moments(moments, wall_flags, wall_temp):
    keep_mask = (jnp.arange(8) == 0).astype(moments.dtype)[:, None, None]
    at_temp = (jnp.arange(8) == 4).astype(moments.dtype)[:, None, None]
    walled = moments * keep_mask + at_temp * wall_temp[None]
    return jnp.where(wall_flags[None] == 1, walled, moments)


def transport(target, padded, speed_x, speed_y, relax_rate):
    along_x = jnp.abs(speed_x)[:, None, None]
    along_y = jnp.abs(speed_y)[:, None, None]
    upwind_x = jnp.where(speed_x[:, None, None] > 0, padded[:, :-2, 1:-1], padded[:, 2:, 1:-1])
    upwind_y = jnp.where(speed_y[:, None, None] > 0, padded[:, 1:-1, :-2], padded[:, 1:-1, 2:])
    return (target * relax_rate + along_x * upwind_x + along_y * upwind_y) / (relax_rate + along_x + along_y)


def operate(grid_field, diagonal):
    padded = jnp.pad(grid_field, 1)
    beside = padded[2:, 1:-1] + padded[:-2, 1:-1] + padded[1:-1, 2:] + padded[1:-1, :-2]
    return (diagonal + 4.0) * grid_field - beside


def conjugate(rhs, diagonal):
    solution = jnp.zeros_like(rhs)
    residual = rhs
    direction = rhs
    norm_now = jnp.sum(residual * residual)
    for rounds in range(ITERS):
        image = operate(direction, diagonal)
        step_size = norm_now / jnp.sum(direction * image)
        solution = solution + step_size * direction
        residual = residual - step_size * image
        norm_next = jnp.sum(residual * residual)
        direction = residual + (norm_next / norm_now) * direction
        norm_now = norm_next
    return solution


def reference(distribution, vel_index, collision_time, wall_flags, wall_temp):
    speed_x, speed_y, moment_rows, shape_rows, temp_shape = velocity_tables(vel_index)
    blocks = N_VEL
    per_block = VEL // blocks
    highest = lax.Precision.HIGHEST
    dist_blocks = distribution.reshape(blocks, per_block, NX, NY)
    rows_blocks = moment_rows.reshape(8, blocks, per_block).transpose(1, 0, 2)
    shape_blocks = shape_rows.reshape(8, blocks, per_block).transpose(1, 0, 2)
    temp_rows = moment_rows[4].reshape(blocks, per_block)
    sx_blocks = speed_x.reshape(blocks, per_block)
    sy_blocks = speed_y.reshape(blocks, per_block)

    def accumulate(carry, pieces):
        rows_piece, dist_piece = pieces
        return carry + jnp.tensordot(rows_piece, dist_piece, axes=1, precision=highest), None

    moments, unused = lax.scan(accumulate, jnp.zeros((8, NX, NY), jnp.float32), (rows_blocks, dist_blocks))
    adjusted = wall_moments(moments, wall_flags, wall_temp)
    relax_rate = 1.0 / collision_time

    def sweep_block(carry, pieces):
        dist_piece, shape_piece, sx_piece, sy_piece, temp_piece = pieces
        target = jnp.tensordot(shape_piece.T, adjusted, axes=1, precision=highest)
        padded = jnp.pad(dist_piece, ((0, 0), (1, 1), (1, 1)))
        swept = transport(target, padded, sx_piece, sy_piece, relax_rate)
        return carry + jnp.tensordot(temp_piece, swept, axes=1, precision=highest), swept

    temp_half, swept_blocks = lax.scan(sweep_block, jnp.zeros((NX, NY), jnp.float32),
                                       (dist_blocks, shape_blocks, sx_blocks, sy_blocks, temp_rows))
    rhs = temp_half - moments[4]
    diagonal = COOLING / collision_time
    correction = conjugate(rhs, diagonal)
    swept_all = swept_blocks.reshape(VEL, NX, NY)
    return swept_all + temp_shape[:, None, None] * correction[None], correction
```

```python
import functools
import math

import jax
import jax.numpy as jnp
import numpy as np
from jax import lax
from jax.experimental import pallas as pl
from jax.experimental.pallas import tpu as pltpu
from jax.sharding import PartitionSpec as P


VGRID = 24
ITERS = 3
VELOCITY_MAX = 4.5
COOLING = 0.08
SHAKHOV = 0.8 * (1.0 - 2.0 / 3.0)
SPACING = 2.0 * VELOCITY_MAX / VGRID
HIGHEST = lax.Precision.HIGHEST
F32 = jnp.float32
LANES = 128
SLOTS = 3456
HALF = SLOTS // 2
BLOCKS = SLOTS // LANES
PAD = HALF + 8
ROWS = 5
CHUNKS = 9
STEP = BLOCKS // CHUNKS
BF16 = jnp.bfloat16


def class_constants():
    axis = -VELOCITY_MAX + (np.arange(VGRID) + 0.5) * SPACING
    sx, sy, sz = (a.reshape(-1) for a in np.meshgrid(axis, axis, axis, indexing="ij"))
    sq = sx * sx + sy * sy + sz * sz
    maxwell = np.exp(-sq) * math.pi**-1.5
    shapes = np.stack(
        [
            maxwell,
            2.0 * sx * maxwell,
            2.0 * sy * maxwell,
            2.0 * sz * maxwell,
            (1.0 - COOLING) * (sq - 1.5) * maxwell,
            SHAKHOV * sx * (sq - 2.5) * maxwell,
            SHAKHOV * sy * (sq - 2.5) * maxwell,
            SHAKHOV * sz * (sq - 2.5) * maxwell,
        ]
    )
    row = SPACING**3 * (2.0 / 3.0 * sq - 1.0)
    n = np.rint((np.abs(sx) + np.abs(sy)) / SPACING).astype(int)
    table = np.zeros((8, VGRID))
    for m in range(8):
        np.add.at(table[m], n, row * shapes[m])
    return table.astype(np.float32)


def iota(shape, dim):
    return lax.broadcasted_iota(jnp.int32, shape, dim)


def fields(slot_ids):
    v = slot_ids.astype(F32)
    index_x = jnp.floor((v + 0.5) * (1.0 / (VGRID * VGRID)))
    rest = v - index_x * (VGRID * VGRID)
    index_y = jnp.floor((rest + 0.5) * (1.0 / VGRID))
    index_z = rest - index_y * VGRID
    sx = -VELOCITY_MAX + (index_x + 0.5) * SPACING
    sy = -VELOCITY_MAX + (index_y + 0.5) * SPACING
    sz = -VELOCITY_MAX + (index_z + 0.5) * SPACING
    n = jnp.abs(index_x - 11.5) + jnp.abs(index_y - 11.5)
    return sx, sy, sz, sx * sx + sy * sy + sz * sz, n


def prefix(x, size, axis):
    place = iota(x.shape, axis)
    step = 1
    while step < size:
        x = x + jnp.where(place >= step, pltpu.roll(x, step, axis), 0)
        step *= 2
    return x


def spread(x, lane):
    return jnp.broadcast_to(x[:, lane : lane + 1], (8, LANES))


def split(x):
    high = x.astype(BF16)
    return high, (x - high.astype(F32)).astype(BF16)


def fetch(pairs, sem):
    copies = [pltpu.make_async_copy(a, b, sem.at[i]) for i, (a, b) in enumerate(pairs)]
    for copy in copies:
        copy.start()
    return copies


def wait(copies):
    for copy in copies:
        copy.wait()


def pieces(source, target, sem, rows):
    def one(c):
        part = pl.ds(pl.multiple_of(c * STEP * rows, 8), STEP * rows)
        return pltpu.make_async_copy(source.at[part], target.at[part], sem.at[c])

    return one


def compact_kernel(f_hbm, v_hbm, up_hbm, down_hbm, dest_hbm, table_hbm,
                   f_ref, v_ref, square, code_t, dest_t, table, buf_p, buf_n, table_s, sem, f_sem):
    read_v = fetch([(v_hbm, v_ref)], sem)
    piece = pieces(f_hbm, f_ref, f_sem, 2 * LANES)
    for c in range(CHUNKS):
        piece(c).start()
    square[...] = jnp.zeros((LANES, LANES), F32)
    wait(read_v)
    square[0:BLOCKS, :] = jnp.where(v_ref[...] >= VGRID**3 // 2, 1.0, 0.0)
    flags = square[...].T
    row = iota((8, LANES), 0)
    dests, signs = [], []
    for a in range(16):
        sign = flags[8 * a : 8 * a + 8, :].astype(jnp.int32)
        running = prefix(sign, 8, 0)
        count = running[7:8, :]
        table[32 + a : 33 + a, :] = count
        ahead = running - sign
        signs.append(sign)
        dests.append(jnp.where(sign > 0, ahead, count + row - ahead))
    count = table[32:48, :]
    within = prefix(count, 16, 0)
    total = jnp.broadcast_to(within[15:16, :], (16, LANES))
    start = prefix(total, 32, 1) - total + within - count
    place = iota((16, LANES), 0) + 16 * iota((16, LANES), 1)
    table[0:16, :] = start
    table[16:32, :] = HALF - (8 * place - start)
    move = fetch([(table, table_s), (table, table_hbm)], sem)
    for a in range(16):
        dest = dests[a]
        dest_t[8 * a : 8 * a + 8, :] = dest.astype(F32)
        code = 8 * signs[a]
        for j in range(1, 8):
            code = code + jnp.where(jnp.broadcast_to(dest[j : j + 1, :], (8, LANES)) == row, j, 0)
        code_t[8 * a : 8 * a + 8, :] = code
    wait(move)
    keep = fetch([(dest_t, dest_hbm)], sem)

    def step(c, carry):
        piece(c).wait()
        codes = pltpu.roll(code_t[...], LANES - STEP * c, 1)
        for i in range(STEP):
            r = STEP * c + i
            for a in range(16):
                at = 256 * r + 16 * a
                first = f_ref[pl.ds(at, 8, stride=2), :]
                last = f_ref[pl.ds(at + 1, 8, stride=2), :]
                code = spread(codes[8 * a : 8 * a + 8, :], i)
                sent = jnp.where(code >= 8, last, first)
                sent = jnp.take_along_axis(sent, code & 7, axis=0)
                buf_p[pl.ds(table_s[a, r], 8), :] = sent
                buf_n[pl.ds(table_s[16 + a, r], 8), :] = sent
        return carry

    lax.fori_loop(0, CHUNKS, step, 0)
    wait(keep)
    wait(fetch([(buf_p.at[0:HALF], up_hbm), (buf_n.at[8:PAD], down_hbm)], sem))


def shift_lanes(x, by):
    lane = iota(x.shape, 1)
    if by > 0:
        return jnp.where(lane == 0, 0.0, pltpu.roll(x, 1, 1))
    return jnp.where(lane == LANES - 1, 0.0, pltpu.roll(x, LANES - 1, 1))


def dot(a, b):
    return jnp.dot(a, b, precision=HIGHEST, preferred_element_type=F32)


def sums_kernel(f_hbm, v_hbm, tau_hbm, before_hbm, after_hbm, wall_hbm, heat_hbm, c_hbm, payload_hbm, moments_hbm,
                f_ref, v_ref, tau_ref, before_ref, after_ref, wall_ref, heat_ref, c_ref, moments_ref, payload, sem, f_sem):
    read_v = fetch([(v_hbm, v_ref)], sem)
    piece = pieces(f_hbm, f_ref, f_sem, 2 * LANES)
    for c in range(CHUNKS):
        piece(c).start()
    wait(read_v)
    others = fetch([(tau_hbm, tau_ref), (before_hbm, before_ref), (after_hbm, after_ref), (wall_hbm, wall_ref),
                    (heat_hbm, heat_ref), (c_hbm, c_ref)], sem)
    weight = SPACING**3
    classes = iota((VGRID, LANES), 0).astype(F32)

    def step(c, sums):
        piece(c).wait()
        for i in range(STEP):
            r = STEP * c + i
            sx, sy, sz, sq, n = fields(v_ref[pl.ds(r, 1), :])
            row_4 = (2.0 / 3.0 * sq - 1.0) * weight
            heat = (sq - 2.5) * weight
            moments = jnp.concatenate(
                [jnp.full_like(sx, weight), sx * weight, sy * weight, sz * weight, row_4, sx * heat, sy * heat, sz * heat], 0
            )
            hot = classes == n
            parts = [moments]
            for speed in (sx, sy):
                along = row_4 * jnp.abs(speed)
                parts.append(jnp.where(hot, jnp.where(speed > 0, along, 0.0), 0.0))
                parts.append(jnp.where(hot, jnp.where(speed > 0, 0.0, along), 0.0))
            high, low = split(jnp.concatenate(parts, 0))
            both = jnp.concatenate([f_ref[pl.ds(256 * r + x, LANES, stride=2), :] for x in range(2)], 1)
            f_high, f_low = split(both)
            sums = sums + jnp.dot(
                jnp.concatenate([high, high, low], 1), jnp.concatenate([f_high, f_low, f_high], 0),
                preferred_element_type=F32,
            )
        return sums

    sums = lax.fori_loop(0, CHUNKS, step, jnp.zeros((8 + 4 * VGRID, 2 * LANES), F32))
    wait(others)

    def part(x, k):
        return sums[8 + VGRID * k : 8 + VGRID * (k + 1), LANES * x : LANES * (x + 1)]

    def inverse(tau):
        return 1.0 / (1.0 / tau + classes * SPACING)

    where_vel = lax.axis_index("vel")
    lead = jnp.where(where_vel == 0, 1.0, 0.0)
    rows = []
    for x in range(2):
        tau = tau_ref[x : x + 1, :]
        inv = inverse(tau)
        kernels = dot(c_ref[...], inv) * (1.0 / tau)
        moments = sums[0:8, LANES * x : LANES * (x + 1)]
        product = moments * kernels
        gas = jnp.sum(product, 0, keepdims=True)
        wall = product[0:1, :] + lead * heat_ref[x : x + 1, :] * kernels[4:5, :]
        held = jnp.where(wall_ref[x : x + 1, :] == 1, wall, gas) - moments[4:5, :]
        across = part(1, 1) if x == 0 else part(0, 0)
        moved = inv * (across + shift_lanes(part(x, 2), 1) + shift_lanes(part(x, 3), -1))
        moments_ref[8 * x : 8 * x + 8, :] = moments
        rows.append(held + jnp.sum(moved, 0, keepdims=True))
    rows.append(jnp.sum(inverse(before_ref[...]) * part(0, 1), 0, keepdims=True))
    rows.append(jnp.sum(inverse(after_ref[...]) * part(1, 0), 0, keepdims=True))
    rows.append(jnp.where(where_vel == 0, tau_ref[0:1, :], tau_ref[1:2, :]))
    for k in range(8):
        for j in range(ROWS):
            payload[ROWS * k + j : ROWS * k + j + 1, :] = rows[j]
    block = payload[0 : 8 * ROWS, :]
    for k in range(1, 32):
        payload[8 * ROWS * k : 8 * ROWS * (k + 1), :] = block
    wait(fetch([(moments_ref, moments_hbm), (payload, payload_hbm)], sem))


def sweep_kernel(f_hbm, v_hbm, mine_hbm, other_hbm, tau_hbm, wall_hbm, heat_hbm, dest_hbm, pre_hbm, along_hbm, shape_hbm, index_hbm,
                 f_ref, v_ref, mine_ref, other_ref, tau_ref, wall_ref, heat_ref, dest_ref, pre_ref, along_ref, shape_ref, index_ref,
                 rhs, cols, sem, f_sem, pre_sem, along_sem, shape_sem, index_sem):
    first = fetch([(v_hbm, v_ref), (mine_hbm, mine_ref), (other_hbm, other_ref), (tau_hbm, tau_ref), (wall_hbm, wall_ref),
                   (heat_hbm, heat_ref), (dest_hbm, dest_ref)], sem)
    piece = pieces(f_hbm, f_ref, f_sem, 2 * LANES)
    for c in range(CHUNKS):
        piece(c).start()
    outs = [pieces(pre_ref, pre_hbm, pre_sem, 2 * LANES), pieces(along_ref, along_hbm, along_sem, LANES),
            pieces(shape_ref, shape_hbm, shape_sem, LANES), pieces(index_ref, index_hbm, index_sem, LANES)]
    rhs[...] = jnp.zeros((LANES, 8 * LANES), F32)
    cols[...] = jnp.zeros((LANES, LANES), F32)
    row = iota((8, LANES), 0)
    classes = iota((VGRID, LANES), 0).astype(F32)
    wait(first)
    dest_ref[...] = dest_ref[...].T
    for x in range(2):
        moments = mine_ref[8 * x : 8 * x + 8, :] + other_ref[8 * x : 8 * x + 8, :]
        wall = jnp.where(row == 0, moments, jnp.where(row == 4, heat_ref[x : x + 1, :], 0.0))
        relax = 1.0 / tau_ref[x : x + 1, :]
        adjusted = jnp.where(wall_ref[x : x + 1, :] == 1, wall, moments)
        high, low = (p.astype(F32) for p in split(adjusted * relax))
        here = slice(LANES * x, LANES * (x + 1))
        rhs[0:8, here] = high
        rhs[8:16, here] = low
        rhs[16:24, here] = high
        high, low = (p.astype(F32) for p in split(1.0 / (relax + classes * SPACING)))
        here = slice(LANES * (2 + x), LANES * (3 + x))
        rhs[24:48, here] = high
        rhs[48:72, here] = low
    for k, rows in enumerate(((0,), (1,), (2, 3), (4,))):
        mask = functools.reduce(jnp.logical_or, [row == j for j in rows])
        rhs[72:80, LANES * (4 + k) : LANES * (5 + k)] = jnp.where(mask, 1.0, 0.0)
    rhs_value = rhs[...].astype(BF16)

    def step(c, carry):
        piece(c).wait()
        for i in range(STEP):
            r = STEP * c + i
            sx, sy, sz, sq, n = fields(v_ref[pl.ds(r, 1), :])
            maxwell = jnp.exp(-sq) * math.pi**-1.5
            shape = (sq - 1.5) * maxwell
            heat = SHAKHOV * (sq - 2.5) * maxwell
            high, low = (p.astype(F32) for p in split(jnp.concatenate(
                [maxwell, 2.0 * sx * maxwell, 2.0 * sy * maxwell, 2.0 * sz * maxwell,
                 (1.0 - COOLING) * shape, sx * heat, sy * heat, sz * heat], 0)))
            shape_high, shape_low = (p.astype(F32) for p in split(shape))
            hot = jnp.where(classes == n, 1.0, 0.0)
            zero = jnp.zeros_like(sx)
            cols[0:80, :] = jnp.concatenate(
                [high, high, low, hot, hot, sx, sy, shape_high, shape_low, dest_ref[pl.ds(r, 1), :], zero, zero, zero], 0)
            made = jnp.dot(cols[...].T.astype(BF16), rhs_value, preferred_element_type=F32)
            speed_x, speed_y = made[:, 4 * LANES : 5 * LANES], made[:, 5 * LANES : 6 * LANES]
            rows = [f_ref[pl.ds(256 * r + x, LANES, stride=2), :] for x in range(2)]
            along_x, along_y = jnp.abs(speed_x), jnp.abs(speed_y)
            ahead = speed_x > 0
            for x in range(2):
                upwind_y = jnp.where(speed_y > 0, shift_lanes(rows[x], 1), shift_lanes(rows[x], -1))
                near = jnp.where(ahead, 0.0, rows[1]) if x == 0 else jnp.where(ahead, rows[0], 0.0)
                inv = made[:, LANES * (2 + x) : LANES * (3 + x)]
                value = (made[:, LANES * x : LANES * (x + 1)] + along_x * near + along_y * upwind_y) * inv
                pre_ref[pl.ds(256 * r + x, LANES, stride=2), :] = value
            at = pl.ds(pl.multiple_of(LANES * r, LANES), LANES)
            along_ref[at, :] = speed_x * jnp.where(ahead, made[:, 2 * LANES : 3 * LANES], made[:, 3 * LANES : 4 * LANES])
            shape_ref[at, :] = made[:, 6 * LANES : 7 * LANES]
            index_ref[at, :] = made[:, 7 * LANES :].astype(jnp.int32)
        for out in outs:
            out(c).start()
        return carry

    lax.fori_loop(0, CHUNKS, step, 0)
    for c in range(CHUNKS):
        for out in outs:
            out(c).wait()


def solve_kernel(y_hbm, out_ref, y_ref, kept, sem):
    wait(fetch([(y_hbm, y_ref)], sem))

    def take(device, j):
        return y_ref[pl.ds(ROWS * device + j, 64, stride=ROWS), :]

    place = iota((64, LANES), 0)

    def lower(x):
        return jnp.where(place == 0, 0.0, pltpu.roll(x, 1, 0))

    def upper(x):
        return jnp.where(place == 63, 0.0, pltpu.roll(x, 63, 0))

    def over_vel(j):
        return take(0, j) + take(64, j) + take(128, j) + take(192, j)

    even = over_vel(0) + lower(over_vel(3))
    odd = over_vel(1) + upper(over_vel(2))
    middle_even = COOLING / take(0, 4) + 4.0
    middle_odd = COOLING / take(64, 4) + 4.0

    def operate(e, o):
        image_e = middle_even * e - (lower(o) + o + shift_lanes(e, 1) + shift_lanes(e, -1))
        image_o = middle_odd * o - (e + upper(e) + shift_lanes(o, 1) + shift_lanes(o, -1))
        return image_e, image_o

    def inner(a, b):
        total = jnp.sum(a[0] * b[0] + a[1] * b[1], 0, keepdims=True)
        return jnp.sum(total, 1, keepdims=True)

    residual = (even, odd)
    direction = residual
    found = (jnp.zeros_like(even), jnp.zeros_like(odd))
    norm_now = inner(residual, residual)
    for rounds in range(ITERS):
        image = operate(*direction)
        step_size = norm_now / inner(direction, image)
        found = tuple(v + step_size * d for v, d in zip(found, direction))
        if rounds + 1 < ITERS:
            residual = tuple(r - step_size * i for r, i in zip(residual, image))
            norm_next = inner(residual, residual)
            direction = tuple(r + norm_next / norm_now * d for r, d in zip(residual, direction))
            norm_now = norm_next
    kept[0:64, :] = found[0]
    kept[64:128, :] = found[1]
    out_ref[0:1, :] = kept[pl.ds(lax.axis_index("space"), 1), :]
    out_ref[1:2, :] = kept[pl.ds(64 + lax.axis_index("space"), 1), :]


def finish_kernel(pre_hbm, along_hbm, shape_hbm, index_hbm, corr_hbm, up_hbm, down_hbm, table_hbm, out_hbm,
                  pre_ref, along_ref, shape_ref, index_ref, corr_ref, buf_p, buf_n, table_s, out_ref,
                  sem, pre_sem, along_sem, shape_sem, index_sem, out_sem):
    first = fetch([(table_hbm, table_s), (corr_hbm, corr_ref), (up_hbm, buf_p.at[0:HALF]), (down_hbm, buf_n.at[8:PAD])], sem)
    ins = [pieces(pre_hbm, pre_ref, pre_sem, 2 * LANES), pieces(along_hbm, along_ref, along_sem, LANES),
           pieces(shape_hbm, shape_ref, shape_sem, LANES), pieces(index_hbm, index_ref, index_sem, LANES)]
    done = pieces(out_ref, out_hbm, out_sem, 2 * LANES)
    for c in range(CHUNKS):
        for piece in ins:
            piece(c).start()
    wait(first)
    corr = [jnp.broadcast_to(corr_ref[x : x + 1, :], (8, LANES)) for x in range(2)]
    row = iota((8, LANES), 0)

    def step(c, carry):
        for piece in ins:
            piece(c).wait()
        for i in range(STEP):
            r = STEP * c + i
            for a in range(16):
                at = 128 * r + 8 * a
                here = pl.ds(pl.multiple_of(at, 8), 8)
                halo = jnp.where(row < table_s[32 + a, r], buf_p[pl.ds(table_s[a, r], 8), :],
                                 buf_n[pl.ds(table_s[16 + a, r], 8), :])
                moved = along_ref[here, :] * jnp.take_along_axis(halo, index_ref[here, :], axis=0)
                ahead = along_ref[here, :] > 0
                shape = shape_ref[here, :]
                near = pl.ds(2 * at, 8, stride=2)
                far = pl.ds(2 * at + 1, 8, stride=2)
                out_ref[near, :] = pre_ref[near, :] + jnp.where(ahead, moved, 0.0) + shape * corr[0]
                out_ref[far, :] = pre_ref[far, :] - jnp.where(ahead, 0.0, moved) + shape * corr[1]
        done(c).start()
        return carry

    lax.fori_loop(0, CHUNKS, step, 0)
    for c in range(CHUNKS):
        done(c).wait()


def vmem(shape, dtype=F32):
    return pltpu.VMEM(shape, dtype)


def struct(shape, dtype=F32):
    return jax.ShapeDtypeStruct(shape, dtype)


IN_HBM = pl.BlockSpec(memory_space=pl.ANY)
IN_VMEM = pl.BlockSpec(memory_space=pltpu.VMEM)
DMA = pltpu.SemaphoreType.DMA
INT = jnp.int32


def call(kernel, outs, scratch, args, flops, out_spec=IN_HBM):
    return pl.pallas_call(
        kernel,
        out_shape=outs,
        in_specs=[IN_HBM] * len(args),
        out_specs=jax.tree.map(lambda _: out_spec, outs),
        scratch_shapes=scratch,
        cost_estimate=pl.CostEstimate(flops=flops, bytes_accessed=8 << 20, transcendentals=0),
    )(*args)


def program(distribution, vel_index, collision_time, wall_flags, wall_temp):
    space = lax.axis_size("space")
    vel = lax.axis_size("vel")
    up = [(i, i + 1) for i in range(space - 1)]
    down = [(j, i) for i, j in up]
    partner = [(i, i ^ 1) for i in range(vel)]
    opposite = [(i, (i + vel // 2) % vel) for i in range(vel)]

    flat = distribution.reshape(2 * SLOTS, LANES)
    ids = vel_index.reshape(BLOCKS, LANES)
    small, square, whole, halves = (2, LANES), (LANES, LANES), (2 * SLOTS, LANES), (SLOTS, LANES)
    before = lax.ppermute(collision_time[1:2], "space", up)
    after = lax.ppermute(collision_time[0:1], "space", down)
    rows_up, rows_down, dest, table = call(
        compact_kernel,
        (struct((HALF, LANES)), struct((HALF, LANES)), struct(square), struct((48, LANES), INT)),
        [vmem(whole), vmem((BLOCKS, LANES), INT), vmem(square), vmem(square, INT), vmem(square), vmem((48, LANES), INT),
         vmem((PAD, LANES)), vmem((PAD, LANES)), pltpu.SMEM((48, LANES), INT), DMA((2,)), DMA((CHUNKS,))],
        (flat, ids), 1 << 20,
    )
    halo_up = lax.ppermute(rows_up, "space", up)
    payload, moments = call(
        sums_kernel, (struct((ROWS * vel * space, LANES)), struct((16, LANES))),
        [vmem(whole), vmem((BLOCKS, LANES), INT), vmem(small), vmem((1, LANES)), vmem((1, LANES)), vmem(small, INT), vmem(small),
         vmem((8, VGRID)), vmem((16, LANES)), vmem((256 * ROWS, LANES)), DMA((6,)), DMA((CHUNKS,))],
        (flat, ids, collision_time, before, after, wall_flags, wall_temp, jnp.asarray(class_constants())), 1 << 30,
    )
    gathered = lax.all_to_all(payload.reshape(vel * space, 1, ROWS * LANES), ("vel", "space"), 0, 0, tiled=True)
    moments = moments + lax.ppermute(moments, "vel", partner)
    moments_other = lax.ppermute(moments, "vel", opposite)
    halo_down = lax.ppermute(rows_down, "space", down)
    pre, along, shape, index = call(
        sweep_kernel,
        (struct(whole), struct(halves), struct(halves), struct(halves, INT)),
        [vmem(whole), vmem((BLOCKS, LANES), INT), vmem((16, LANES)), vmem((16, LANES)), vmem(small), vmem(small, INT), vmem(small),
         vmem(square), vmem(whole), vmem(halves), vmem(halves), vmem(halves, INT), vmem((LANES, 8 * LANES)), vmem(square),
         DMA((7,)), DMA((CHUNKS,)), DMA((CHUNKS,)), DMA((CHUNKS,)), DMA((CHUNKS,)), DMA((CHUNKS,))],
        (flat, ids, moments, moments_other, collision_time, wall_flags, wall_temp, dest), 1 << 30,
    )
    correction = call(
        solve_kernel, struct(small), [vmem((ROWS * vel * space, LANES)), vmem(square), DMA((1,))],
        (gathered.reshape(ROWS * vel * space, LANES),), 1 << 24, IN_VMEM,
    )
    result = call(
        finish_kernel, struct(whole),
        [vmem(whole), vmem(halves), vmem(halves), vmem(halves, INT), vmem(small), vmem((PAD, LANES)), vmem((PAD, LANES)),
         pltpu.SMEM((48, LANES), INT), vmem(whole), DMA((4,))] + [DMA((CHUNKS,))] * 5,
        (pre, along, shape, index, correction, halo_up, halo_down, table), 1 << 24,
    )
    return result.reshape(SLOTS, 2, LANES), correction


def solution(mesh):
    placed = (
        P("vel", "space", None),
        P("vel"),
        P("space", None),
        P("space", None),
        P("space", None),
    )
    return jax.shard_map(
        program,
        mesh=mesh,
        in_specs=placed,
        out_specs=(P("vel", "space", None), P("space", None)),
        check_vma=False,
    )
```

```python
import math

import jax
import jax.numpy as jnp
import numpy as np
from jax import lax
from jax.experimental import pallas as pl
from jax.experimental.pallas import tpu as pltpu
from jax.sharding import PartitionSpec as P


VGRID = 24
ITERS = 3
VELOCITY_MAX = 4.5
COOLING = 0.08
SHAKHOV = 0.8 * (1.0 - 2.0 / 3.0)
SPACING = 2.0 * VELOCITY_MAX / VGRID
HIGHEST = lax.Precision.HIGHEST
F32 = jnp.float32
LANES = 128
SLOTS = 3456
HALF = SLOTS // 2
BLOCKS = SLOTS // LANES
PAD = HALF + 8
ROWS = 6
EARLY = 1000
CHUNKS = 9
STEP = BLOCKS // CHUNKS
BF16 = jnp.bfloat16


def class_constants():
    axis = -VELOCITY_MAX + (np.arange(VGRID) + 0.5) * SPACING
    sx, sy, sz = (a.reshape(-1) for a in np.meshgrid(axis, axis, axis, indexing="ij"))
    sq = sx * sx + sy * sy + sz * sz
    maxwell = np.exp(-sq) * math.pi**-1.5
    shapes = np.stack(
        [
            maxwell,
            2.0 * sx * maxwell,
            2.0 * sy * maxwell,
            2.0 * sz * maxwell,
            (1.0 - COOLING) * (sq - 1.5) * maxwell,
            SHAKHOV * sx * (sq - 2.5) * maxwell,
            SHAKHOV * sy * (sq - 2.5) * maxwell,
            SHAKHOV * sz * (sq - 2.5) * maxwell,
        ]
    )
    row = SPACING**3 * (2.0 / 3.0 * sq - 1.0)
    n = np.rint((np.abs(sx) + np.abs(sy)) / SPACING).astype(int)
    table = np.zeros((8, VGRID))
    for m in range(8):
        np.add.at(table[m], n, row * shapes[m])
    return table.astype(np.float32)


def iota(shape, dim):
    return lax.broadcasted_iota(jnp.int32, shape, dim)


def fields(slot_ids):
    v = slot_ids.astype(F32)
    index_x = jnp.floor((v + 0.5) * (1.0 / (VGRID * VGRID)))
    rest = v - index_x * (VGRID * VGRID)
    index_y = jnp.floor((rest + 0.5) * (1.0 / VGRID))
    index_z = rest - index_y * VGRID
    sx = -VELOCITY_MAX + (index_x + 0.5) * SPACING
    sy = -VELOCITY_MAX + (index_y + 0.5) * SPACING
    sz = -VELOCITY_MAX + (index_z + 0.5) * SPACING
    n = jnp.abs(index_x - 11.5) + jnp.abs(index_y - 11.5)
    return sx, sy, sz, sx * sx + sy * sy + sz * sz, n


def spread(x, lane):
    return jnp.broadcast_to(x[:, lane : lane + 1], (8, LANES))


def split(x):
    high = x.astype(BF16)
    return high, (x - high.astype(F32)).astype(BF16)


def fetch(pairs, sem):
    copies = [pltpu.make_async_copy(a, b, sem.at[i]) for i, (a, b) in enumerate(pairs)]
    for copy in copies:
        copy.start()
    return copies


def wait(copies):
    for copy in copies:
        copy.wait()


def pieces(source, target, sem, rows):
    def one(c):
        part = pl.ds(pl.multiple_of(c * STEP * rows, 8), STEP * rows)
        return pltpu.make_async_copy(source.at[part], target.at[part], sem.at[c])

    return one


def compact_kernel(f_hbm, v_hbm, up_hbm, early_hbm, late_hbm, dest_hbm, table_hbm,
                   f_ref, v_ref, square, code_t, dest_t, table, buf_p, buf_n, table_s, sem, f_sem):
    read_v = fetch([(v_hbm, v_ref)], sem)
    piece = pieces(f_hbm, f_ref, f_sem, 2 * LANES)
    for c in range(CHUNKS):
        piece(c).start()
    square[...] = jnp.zeros((LANES, LANES), F32)
    down, along = iota((LANES, LANES), 0), iota((LANES, LANES), 1)
    inside = jnp.where((down // 8 == along // 8) & (along < down), 1.0, 0.0).astype(BF16)
    group = iota((16, LANES), 0)
    before = jnp.where(iota((16, LANES), 1) // 8 < group, 1.0, 0.0).astype(BF16)
    within = jnp.where(iota((16, LANES), 1) // 8 == group, 1.0, 0.0).astype(BF16)
    earlier = jnp.where(down < along, 1.0, 0.0).astype(BF16)
    wait(read_v)
    square[0:BLOCKS, :] = jnp.where(v_ref[...] >= VGRID**3 // 2, 1.0, 0.0)
    flags = square[...].T

    def count_of(a, b):
        return jnp.dot(a, b, preferred_element_type=F32)

    marks = flags.astype(BF16)
    count = count_of(within, marks)
    total = jnp.sum(count, 0, keepdims=True)
    start = count_of(before, marks) + count_of(jnp.broadcast_to(total, (16, LANES)).astype(BF16), earlier)
    start = start.astype(jnp.int32)
    place = iota((16, LANES), 0) + 16 * iota((16, LANES), 1)
    table[0:16, :] = start
    table[16:32, :] = HALF - (8 * place - start)
    table[32:48, :] = count.astype(jnp.int32)
    move = fetch([(table, table_s), (table, table_hbm)], sem)
    ranks = count_of(inside, marks)
    row = iota((8, LANES), 0)
    dests, signs = [], []
    for a in range(16):
        sign = flags[8 * a : 8 * a + 8, :].astype(jnp.int32)
        ahead = ranks[8 * a : 8 * a + 8, :].astype(jnp.int32)
        signs.append(sign)
        dests.append(jnp.where(sign > 0, ahead, table[32 + a : 33 + a, :] + row - ahead))
    for a in range(16):
        dest = dests[a]
        dest_t[8 * a : 8 * a + 8, :] = dest
        code = 8 * signs[a]
        for j in range(1, 8):
            code = code + jnp.where(jnp.broadcast_to(dest[j : j + 1, :], (8, LANES)) == row, j, 0)
        code_t[8 * a : 8 * a + 8, :] = code
    wait(move)
    keep = fetch([(dest_t, dest_hbm)], sem)

    def step(c, carry):
        piece(c).wait()
        codes = pltpu.roll(code_t[...], LANES - STEP * c, 1)
        for i in range(STEP):
            r = STEP * c + i
            for a in range(16):
                at = 256 * r + 16 * a
                first = f_ref[pl.ds(at, 8, stride=2), :]
                last = f_ref[pl.ds(at + 1, 8, stride=2), :]
                code = spread(codes[8 * a : 8 * a + 8, :], i)
                sent = jnp.where(code >= 8, last, first)
                sent = jnp.take_along_axis(sent, code & 7, axis=0)
                buf_p[pl.ds(table_s[a, r], 8), :] = sent
                buf_n[pl.ds(table_s[16 + a, r], 8), :] = sent
        return carry

    lax.fori_loop(0, CHUNKS, step, 0)
    wait(fetch([(buf_p, up_hbm), (buf_n.at[PAD - EARLY : PAD], early_hbm), (buf_n.at[0 : PAD - EARLY], late_hbm)], f_sem))
    wait(keep)


def shift_lanes(x, by):
    lane = iota(x.shape, 1)
    if by > 0:
        return jnp.where(lane == 0, 0.0, pltpu.roll(x, 1, 1))
    return jnp.where(lane == LANES - 1, 0.0, pltpu.roll(x, LANES - 1, 1))


def dot(a, b):
    return jnp.dot(a, b, precision=HIGHEST, preferred_element_type=F32)


def sums_kernel(f_hbm, v_hbm, tau_hbm, side_ref, other_ref, wall_hbm, heat_hbm, c_hbm, out_hbm,
                f_ref, v_ref, tau_ref, wall_ref, heat_ref, c_ref, out_ref, sem, f_sem):
    read_v = fetch([(v_hbm, v_ref)], sem)
    piece = pieces(f_hbm, f_ref, f_sem, 2 * LANES)
    for c in range(CHUNKS):
        piece(c).start()
    wait(read_v)
    others = fetch([(tau_hbm, tau_ref), (wall_hbm, wall_ref), (heat_hbm, heat_ref), (c_hbm, c_ref)], sem)
    weight = SPACING**3
    classes = iota((VGRID, LANES), 0).astype(F32)

    def step(c, sums):
        piece(c).wait()
        for i in range(STEP):
            r = STEP * c + i
            sx, sy, sz, sq, n = fields(v_ref[pl.ds(r, 1), :])
            row_4 = (2.0 / 3.0 * sq - 1.0) * weight
            heat = (sq - 2.5) * weight
            moments = jnp.concatenate(
                [jnp.full_like(sx, weight), sx * weight, sy * weight, sz * weight, row_4, sx * heat, sy * heat, sz * heat], 0
            )
            hot = classes == n
            parts = [moments]
            for speed in (sx, sy):
                along = row_4 * jnp.abs(speed)
                parts.append(jnp.where(hot, jnp.where(speed > 0, along, 0.0), 0.0))
                parts.append(jnp.where(hot, jnp.where(speed > 0, 0.0, along), 0.0))
            high, low = split(jnp.concatenate(parts, 0))
            both = jnp.concatenate([f_ref[pl.ds(256 * r + x, LANES, stride=2), :] for x in range(2)], 1)
            f_high, f_low = split(both)
            sums = sums + jnp.dot(
                jnp.concatenate([high, high, low], 1), jnp.concatenate([f_high, f_low, f_high], 0),
                preferred_element_type=F32,
            )
        return sums

    sums = lax.fori_loop(0, CHUNKS, step, jnp.zeros((8 + 4 * VGRID, 2 * LANES), F32))
    wait(others)

    def part(x, k):
        return sums[8 + VGRID * k : 8 + VGRID * (k + 1), LANES * x : LANES * (x + 1)]

    def inverse(tau):
        return 1.0 / (1.0 / tau + classes * SPACING)

    where_vel = 2 * lax.axis_index("chip") + lax.axis_index("core")
    lead = jnp.where(where_vel == 0, 1.0, 0.0)
    core = lax.rem(where_vel, 2)
    before = jnp.where(core == 0, side_ref[1:2, :], other_ref[1:2, :])
    after = jnp.where(core == 0, other_ref[0:1, :], side_ref[0:1, :])
    rows = []
    for x in range(2):
        tau = tau_ref[x : x + 1, :]
        inv = inverse(tau)
        kernels = dot(c_ref[...], inv) * (1.0 / tau)
        moments = sums[0:8, LANES * x : LANES * (x + 1)]
        product = moments * kernels
        gas = jnp.sum(product, 0, keepdims=True)
        wall = product[0:1, :] + lead * heat_ref[x : x + 1, :] * kernels[4:5, :]
        held = jnp.where(wall_ref[x : x + 1, :] == 1, wall, gas) - moments[4:5, :]
        across = part(1, 1) if x == 0 else part(0, 0)
        moved = inv * (across + shift_lanes(part(x, 2), 1) + shift_lanes(part(x, 3), -1))
        out_ref[8 * x : 8 * x + 8, :] = moments
        rows.append(held + jnp.sum(moved, 0, keepdims=True))
    rows.append(jnp.sum(inverse(before) * part(0, 1), 0, keepdims=True))
    rows.append(jnp.sum(inverse(after) * part(1, 0), 0, keepdims=True))
    for j in range(4):
        out_ref[16 + j : 17 + j, :] = rows[j]
    out_ref[20:24, :] = jnp.zeros((4, LANES), F32)
    wait(fetch([(out_ref, out_hbm)], sem))


def merge_kernel(mine_hbm, other_hbm, tau_hbm, payload_hbm, moments_hbm, mine_ref, other_ref, tau_ref, moments_ref, payload, sem):
    wait(fetch([(mine_hbm, mine_ref), (other_hbm, other_ref), (tau_hbm, tau_ref)], sem))
    both = mine_ref[...] + other_ref[...]
    moments_ref[...] = both[0:16, :]
    for k in range(4):
        payload[ROWS * k : ROWS * k + 4, :] = both[16:20, :]
        payload[ROWS * k + 4 : ROWS * k + 6, :] = tau_ref[...]
    block = payload[0 : 4 * ROWS, :]
    for k in range(1, payload.shape[0] // (4 * ROWS)):
        payload[4 * ROWS * k : 4 * ROWS * (k + 1), :] = block
    wait(fetch([(moments_ref, moments_hbm), (payload, payload_hbm)], sem))


def sweep_kernel(f_hbm, v_hbm, mine_hbm, other_hbm, tau_hbm, wall_hbm, heat_hbm, pre_hbm, along_hbm, shape_hbm,
                 f_ref, v_ref, mine_ref, other_ref, tau_ref, wall_ref, heat_ref, pre_ref, along_ref, shape_ref,
                 rhs, cols, sem, f_sem, pre_sem, along_sem):
    first = fetch([(v_hbm, v_ref), (mine_hbm, mine_ref), (other_hbm, other_ref), (tau_hbm, tau_ref), (wall_hbm, wall_ref),
                   (heat_hbm, heat_ref)], sem)
    piece = pieces(f_hbm, f_ref, f_sem, 2 * LANES)
    for c in range(CHUNKS):
        piece(c).start()
    outs = [pieces(pre_ref, pre_hbm, pre_sem, 2 * LANES), pieces(along_ref, along_hbm, along_sem, LANES)]
    rhs[...] = jnp.zeros((LANES, 6 * LANES), F32)
    shape_ref[...] = jnp.zeros((LANES, LANES), F32)
    cols[...] = jnp.zeros((LANES, LANES), F32)
    row = iota((8, LANES), 0)
    classes = iota((VGRID, LANES), 0).astype(F32)
    wait(first)
    for x in range(2):
        part = slice(8 * x, 8 * x + 8)
        moments = mine_ref[part, :] + other_ref[part, :]
        wall = jnp.where(row == 0, moments, jnp.where(row == 4, heat_ref[x : x + 1, :], 0.0))
        relax = 1.0 / tau_ref[x : x + 1, :]
        adjusted = jnp.where(wall_ref[x : x + 1, :] == 1, wall, moments)
        high, low = (p.astype(F32) for p in split(adjusted * relax))
        here = slice(LANES * x, LANES * (x + 1))
        rhs[0:8, here] = high
        rhs[8:16, here] = low
        rhs[16:24, here] = high
        high, low = (p.astype(F32) for p in split(1.0 / (relax + classes * SPACING)))
        here = slice(LANES * (2 + x), LANES * (3 + x))
        rhs[24:48, here] = high
        rhs[48:72, here] = low
    for k in range(2):
        rhs[72:80, LANES * (4 + k) : LANES * (5 + k)] = jnp.where(row == k, 1.0, 0.0)
    rhs_value = rhs[...].astype(BF16)

    def step(c, carry):
        piece(c).wait()
        for i in range(STEP):
            r = STEP * c + i
            sx, sy, sz, sq, n = fields(v_ref[pl.ds(r, 1), :])
            maxwell = jnp.exp(-sq) * math.pi**-1.5
            shape = (sq - 1.5) * maxwell
            heat = SHAKHOV * (sq - 2.5) * maxwell
            high, low = (p.astype(F32) for p in split(jnp.concatenate(
                [maxwell, 2.0 * sx * maxwell, 2.0 * sy * maxwell, 2.0 * sz * maxwell,
                 (1.0 - COOLING) * shape, sx * heat, sy * heat, sz * heat], 0)))
            shape_ref[pl.ds(r, 1), :] = shape
            hot = jnp.where(classes == n, 1.0, 0.0)
            zero = jnp.zeros_like(sx)
            cols[0:80, :] = jnp.concatenate(
                [high, high, low, hot, hot, sx, sy, zero, zero, zero, zero, zero, zero], 0)
            made = jnp.dot(cols[...].T.astype(BF16), rhs_value, preferred_element_type=F32)
            speed_x, speed_y = made[:, 4 * LANES : 5 * LANES], made[:, 5 * LANES : 6 * LANES]
            rows = [f_ref[pl.ds(256 * r + x, LANES, stride=2), :] for x in range(2)]
            along_x, along_y = jnp.abs(speed_x), jnp.abs(speed_y)
            ahead = speed_x > 0
            for x in range(2):
                upwind_y = jnp.where(speed_y > 0, shift_lanes(rows[x], 1), shift_lanes(rows[x], -1))
                near = jnp.where(ahead, 0.0, rows[1]) if x == 0 else jnp.where(ahead, rows[0], 0.0)
                inv = made[:, LANES * (2 + x) : LANES * (3 + x)]
                value = (made[:, LANES * x : LANES * (x + 1)] + along_x * near + along_y * upwind_y) * inv
                pre_ref[pl.ds(256 * r + x, LANES, stride=2), :] = value
            at = pl.ds(pl.multiple_of(LANES * r, LANES), LANES)
            along_ref[at, :] = speed_x * jnp.where(ahead, made[:, 2 * LANES : 3 * LANES], made[:, 3 * LANES : 4 * LANES])
        for out in outs:
            out(c).start()
        return carry

    lax.fori_loop(0, CHUNKS, step, 0)
    shape_ref[...] = shape_ref[...].T
    keep = fetch([(shape_ref, shape_hbm)], sem)
    wait(keep)
    for c in range(CHUNKS):
        for out in outs:
            out(c).wait()


def finish_kernel(pre_hbm, along_hbm, shape_hbm, dest_hbm, table_hbm, y_hbm, up_hbm, early_hbm, late_hbm, out_hbm, corr_ref,
                  pre_ref, along_ref, shape_t, dest_t, table_s, y_ref, buf_p, buf_n, kept, out_ref, sem, pre_sem, along_sem, out_sem):
    copies = fetch([(y_hbm, y_ref), (table_hbm, table_s), (shape_hbm, shape_t), (dest_hbm, dest_t), (up_hbm, buf_p),
                    (early_hbm, buf_n.at[PAD - EARLY : PAD]), (late_hbm, buf_n.at[0 : PAD - EARLY])], sem)
    ins = [pieces(pre_hbm, pre_ref, pre_sem, 2 * LANES), pieces(along_hbm, along_ref, along_sem, LANES)]
    done = pieces(out_ref, out_hbm, out_sem, 2 * LANES)
    for c in range(CHUNKS):
        for piece in ins:
            piece(c).start()
    copies[0].wait()

    def take(device, j):
        return y_ref[pl.ds(ROWS * device + j, 64, stride=ROWS), :]

    place = iota((64, LANES), 0)

    def lower(x):
        return jnp.where(place == 0, 0.0, pltpu.roll(x, 1, 0))

    def upper(x):
        return jnp.where(place == 63, 0.0, pltpu.roll(x, 63, 0))

    def over_vel(j):
        return take(0, j) + take(64, j)

    even = over_vel(0) + lower(over_vel(3))
    odd = over_vel(1) + upper(over_vel(2))
    middle_even = COOLING / take(0, 4) + 4.0
    middle_odd = COOLING / take(0, 5) + 4.0

    def operate(e, o):
        image_e = middle_even * e - (lower(o) + o + shift_lanes(e, 1) + shift_lanes(e, -1))
        image_o = middle_odd * o - (e + upper(e) + shift_lanes(o, 1) + shift_lanes(o, -1))
        return image_e, image_o

    def inner(a, b):
        total = jnp.sum(a[0] * b[0] + a[1] * b[1], 0, keepdims=True)
        return jnp.sum(total, 1, keepdims=True)

    residual = (even, odd)
    direction = residual
    found = (jnp.zeros_like(even), jnp.zeros_like(odd))
    norm_now = inner(residual, residual)
    for rounds in range(ITERS):
        image = operate(*direction)
        step_size = norm_now / inner(direction, image)
        found = tuple(v + step_size * d for v, d in zip(found, direction))
        if rounds + 1 < ITERS:
            residual = tuple(r - step_size * i for r, i in zip(residual, image))
            norm_next = inner(residual, residual)
            direction = tuple(r + norm_next / norm_now * d for r, d in zip(residual, direction))
            norm_now = norm_next
    kept[0:64, :] = found[0]
    kept[64:128, :] = found[1]
    where_space = lax.axis_index("space")
    corr_ref[0:1, :] = kept[pl.ds(where_space, 1), :]
    corr_ref[1:2, :] = kept[pl.ds(64 + where_space, 1), :]
    wait(copies[1:])
    corr = [jnp.broadcast_to(corr_ref[x : x + 1, :], (8, LANES)) for x in range(2)]
    row = iota((8, LANES), 0)

    def step(c, carry):
        for piece in ins:
            piece(c).wait()
        shapes = pltpu.roll(shape_t[...], LANES - STEP * c, 1)
        dests = pltpu.roll(dest_t[...], LANES - STEP * c, 1)
        for i in range(STEP):
            r = STEP * c + i
            for a in range(16):
                at = 128 * r + 8 * a
                here = pl.ds(pl.multiple_of(at, 8), 8)
                halo = jnp.where(row < table_s[32 + a, r], buf_p[pl.ds(table_s[a, r], 8), :],
                                 buf_n[pl.ds(table_s[16 + a, r], 8), :])
                along = along_ref[here, :]
                moved = along * jnp.take_along_axis(halo, spread(dests[8 * a : 8 * a + 8, :], i), axis=0)
                ahead = along > 0
                shape = spread(shapes[8 * a : 8 * a + 8, :], i)
                near = pl.ds(2 * at, 8, stride=2)
                far = pl.ds(2 * at + 1, 8, stride=2)
                out_ref[near, :] = pre_ref[near, :] + jnp.where(ahead, moved, 0.0) + shape * corr[0]
                out_ref[far, :] = pre_ref[far, :] - jnp.where(ahead, 0.0, moved) + shape * corr[1]
        done(c).start()
        return carry

    lax.fori_loop(0, CHUNKS, step, 0)
    for c in range(CHUNKS):
        done(c).wait()


def vmem(shape, dtype=F32):
    return pltpu.VMEM(shape, dtype)


def struct(shape, dtype=F32):
    return jax.ShapeDtypeStruct(shape, dtype)


IN_HBM = pl.BlockSpec(memory_space=pltpu.HBM)
IN_VMEM = pl.BlockSpec(memory_space=pltpu.VMEM)
DMA = pltpu.SemaphoreType.DMA
INT = jnp.int32


def call(kernel, outs, scratch, args, flops, out_specs=None, local=(), mib=None, alias=None):
    return pl.pallas_call(
        kernel,
        out_shape=outs,
        in_specs=[IN_VMEM if i in local else IN_HBM for i in range(len(args))],
        out_specs=jax.tree.map(lambda _: IN_HBM, outs) if out_specs is None else out_specs,
        scratch_shapes=scratch,
        input_output_aliases=alias or {},
        compiler_params=pltpu.CompilerParams(vmem_limit_bytes=None if mib is None else mib << 20),
        cost_estimate=pl.CostEstimate(flops=flops, bytes_accessed=8 << 20, transcendentals=0),
    )(*args)


def program(distribution, vel_index, collision_time, wall_flags, wall_temp):
    space = lax.axis_size("space")
    chips = lax.axis_size("chip")
    up = [(i, i + 1) for i in range(space - 1)]
    down = [(j, i) for i, j in up]
    both = []
    for v in range(2 * chips):
        both += [(v * space + i, v * space + j) for i, j in (up if v % 2 == 0 else down)]

    swap = [(0, 1), (1, 0)]
    ring = []
    for c in range(chips):
        for k in range(space):
            ring.append((c * space + k, c * space + k + 1 if k % 2 == 0 else (c + 1) % chips * space + k - 1))
    flat = distribution.reshape(2 * SLOTS, LANES)
    ids = vel_index.reshape(BLOCKS, LANES)
    small, square, whole, halves = (2, LANES), (LANES, LANES), (2 * SLOTS, LANES), (SLOTS, LANES)
    side = lax.ppermute(collision_time, ("chip", "core", "space"), both)
    rows_up, rows_early, rows_late, dest, table = call(
        compact_kernel,
        (struct((PAD, LANES)), struct((EARLY, LANES)), struct((PAD - EARLY, LANES)), struct(square, INT), struct((48, LANES), INT)),
        [vmem(whole), vmem((BLOCKS, LANES), INT), vmem(square), vmem(square, INT), vmem(square, INT), vmem((48, LANES), INT),
         vmem((PAD, LANES)), vmem((PAD, LANES)), pltpu.SMEM((48, LANES), INT), DMA((2,)), DMA((CHUNKS,))],
        (flat, ids), 1 << 20,
    )
    halo_up = lax.ppermute(rows_up, "space", up)
    halo_early = lax.ppermute(rows_early, "space", down)
    side_other = lax.ppermute(side, "core", swap)
    sums = call(
        sums_kernel, struct((24, LANES)),
        [vmem(whole), vmem((BLOCKS, LANES), INT), vmem(small), vmem(small, INT), vmem(small),
         vmem((8, VGRID)), vmem((24, LANES)), DMA((4,)), DMA((CHUNKS,))],
        (flat, ids, collision_time, side, side_other, wall_flags, wall_temp, jnp.asarray(class_constants())), 1 << 30,
        local=(3, 4),
    )
    sums_other = lax.ppermute(sums, "core", swap)
    gather = ROWS * chips * space
    payload, moments = call(
        merge_kernel, (struct((gather, LANES)), struct((16, LANES))),
        [vmem((24, LANES)), vmem((24, LANES)), vmem(small), vmem((16, LANES)), vmem((gather, LANES)), DMA((3,))],
        (sums, sums_other, collision_time), 1 << 16,
    )
    gathered = lax.all_to_all(payload.reshape(chips * space, 1, ROWS * LANES), ("chip", "space"), 0, 0, tiled=True)
    moments_other = lax.ppermute(lax.ppermute(moments, ("chip", "space"), ring), ("chip", "space"), ring)
    halo_late = lax.ppermute(rows_late, "space", down)
    pre, along, shape = call(
        sweep_kernel,
        (struct(whole), struct(halves), struct(square)),
        [vmem(whole), vmem((BLOCKS, LANES), INT), vmem((16, LANES)), vmem((16, LANES)), vmem(small), vmem(small, INT), vmem(small),
         vmem(whole), vmem(halves), vmem(square), vmem((LANES, 6 * LANES)), vmem(square),
         DMA((6,)), DMA((CHUNKS,)), DMA((CHUNKS,)), DMA((CHUNKS,))],
        (flat, ids, moments, moments_other, collision_time, wall_flags, wall_temp), 1 << 30,
    )
    result, correction = call(
        finish_kernel, (struct(whole), struct(small)),
        [vmem(whole), vmem(halves), vmem(square), vmem(square, INT), pltpu.SMEM((48, LANES), INT), vmem((gather, LANES)),
         vmem((PAD, LANES)), vmem((PAD, LANES)), vmem(square), vmem(whole), DMA((7,))] + [DMA((CHUNKS,))] * 3,
        (pre, along, shape, dest, table, gathered.reshape(gather, LANES), halo_up, halo_early, halo_late), 1 << 24,
        (IN_HBM, IN_VMEM),
    )
    return result.reshape(SLOTS, 2, LANES), correction


def solution(mesh):
    vel, space = mesh.devices.shape
    mesh = jax.sharding.Mesh(mesh.devices.reshape(vel // 2, 2, space), ("chip", "core", "space"))
    cores = ("chip", "core")
    placed = (P(cores, "space", None), P(cores), P("space", None), P("space", None), P("space", None))
    return jax.shard_map(
        program,
        mesh=mesh,
        in_specs=placed,
        out_specs=(P(cores, "space", None), P("space", None)),
        check_vma=False,
    )
```

```python
import math

import jax
import jax.numpy as jnp
import numpy as np
from jax import lax
from jax.experimental import pallas as pl
from jax.experimental.pallas import tpu as pltpu
from jax.sharding import PartitionSpec as P


VGRID = 24
ITERS = 3
VELOCITY_MAX = 4.5
COOLING = 0.08
SHAKHOV = 0.8 * (1.0 - 2.0 / 3.0)
SPACING = 2.0 * VELOCITY_MAX / VGRID
HIGHEST = lax.Precision.HIGHEST
F32 = jnp.float32
LANES = 128
SLOTS = 3456
HALF = SLOTS // 2
BLOCKS = SLOTS // LANES
PAD = HALF + 8
ROWS = 6
EARLY = 760
THIRD = 520
CHUNKS = 9
STEP = BLOCKS // CHUNKS
BF16 = jnp.bfloat16


def class_constants():
    axis = -VELOCITY_MAX + (np.arange(VGRID) + 0.5) * SPACING
    sx, sy, sz = (a.reshape(-1) for a in np.meshgrid(axis, axis, axis, indexing="ij"))
    sq = sx * sx + sy * sy + sz * sz
    maxwell = np.exp(-sq) * math.pi**-1.5
    shapes = np.stack(
        [
            maxwell,
            2.0 * sx * maxwell,
            2.0 * sy * maxwell,
            2.0 * sz * maxwell,
            (1.0 - COOLING) * (sq - 1.5) * maxwell,
            SHAKHOV * sx * (sq - 2.5) * maxwell,
            SHAKHOV * sy * (sq - 2.5) * maxwell,
            SHAKHOV * sz * (sq - 2.5) * maxwell,
        ]
    )
    row = SPACING**3 * (2.0 / 3.0 * sq - 1.0)
    n = np.rint((np.abs(sx) + np.abs(sy)) / SPACING).astype(int)
    table = np.zeros((8, VGRID))
    for m in range(8):
        np.add.at(table[m], n, row * shapes[m])
    return table.astype(np.float32)


def iota(shape, dim):
    return lax.broadcasted_iota(jnp.int32, shape, dim)


def fields(slot_ids):
    v = slot_ids.astype(F32)
    index_x = jnp.floor((v + 0.5) * (1.0 / (VGRID * VGRID)))
    rest = v - index_x * (VGRID * VGRID)
    index_y = jnp.floor((rest + 0.5) * (1.0 / VGRID))
    index_z = rest - index_y * VGRID
    sx = -VELOCITY_MAX + (index_x + 0.5) * SPACING
    sy = -VELOCITY_MAX + (index_y + 0.5) * SPACING
    sz = -VELOCITY_MAX + (index_z + 0.5) * SPACING
    n = jnp.abs(index_x - 11.5) + jnp.abs(index_y - 11.5)
    return sx, sy, sz, sx * sx + sy * sy + sz * sz, n


def spread(x, lane):
    return jnp.broadcast_to(x[:, lane : lane + 1], (8, LANES))


def split(x):
    high = x.astype(BF16)
    return high, (x - high.astype(F32)).astype(BF16)


def fetch(pairs, sem):
    copies = [pltpu.make_async_copy(a, b, sem.at[i]) for i, (a, b) in enumerate(pairs)]
    for copy in copies:
        copy.start()
    return copies


def wait(copies):
    for copy in copies:
        copy.wait()


def pieces(source, target, sem, rows):
    def one(c):
        part = pl.ds(pl.multiple_of(c * STEP * rows, 8), STEP * rows)
        return pltpu.make_async_copy(source.at[part], target.at[part], sem.at[c])

    return one


def compact_kernel(f_hbm, v_hbm, up_hbm, early_hbm, late_hbm, dest_hbm, table_hbm,
                   f_ref, v_ref, square, code_t, dest_t, table, buf_p, buf_n, table_s, sem, f_sem, out_sem):
    read_v = fetch([(v_hbm, v_ref)], sem)
    piece = pieces(f_hbm, f_ref, f_sem, 2 * LANES)
    for c in range(CHUNKS):
        piece(c).start()
    square[...] = jnp.zeros((LANES, LANES), F32)
    down, along = iota((LANES, LANES), 0), iota((LANES, LANES), 1)
    inside = jnp.where((down // 8 == along // 8) & (along < down), 1.0, 0.0).astype(BF16)
    group = iota((16, LANES), 0)
    before = jnp.where(iota((16, LANES), 1) // 8 < group, 1.0, 0.0).astype(BF16)
    within = jnp.where(iota((16, LANES), 1) // 8 == group, 1.0, 0.0).astype(BF16)
    earlier = jnp.where(down < along, 1.0, 0.0).astype(BF16)
    wait(read_v)
    square[0:BLOCKS, :] = jnp.where(v_ref[...] >= VGRID**3 // 2, 1.0, 0.0)
    flags = square[...].T

    def count_of(a, b):
        return jnp.dot(a, b, preferred_element_type=F32)

    marks = flags.astype(BF16)
    count = count_of(within, marks)
    total = jnp.sum(count, 0, keepdims=True)
    start = count_of(before, marks) + count_of(jnp.broadcast_to(total, (16, LANES)).astype(BF16), earlier)
    start = start.astype(jnp.int32)
    place = iota((16, LANES), 0) + 16 * iota((16, LANES), 1)
    table[0:16, :] = start
    table[16:32, :] = HALF - (8 * place - start)
    table[32:48, :] = count.astype(jnp.int32)
    move = fetch([(table, table_s), (table, table_hbm)], sem)
    ranks = count_of(inside, marks)
    row = iota((8, LANES), 0)
    dests, signs = [], []
    for a in range(16):
        sign = flags[8 * a : 8 * a + 8, :].astype(jnp.int32)
        ahead = ranks[8 * a : 8 * a + 8, :].astype(jnp.int32)
        signs.append(sign)
        dests.append(jnp.where(sign > 0, ahead, table[32 + a : 33 + a, :] + row - ahead))
    for a in range(16):
        dest = dests[a]
        dest_t[8 * a : 8 * a + 8, :] = dest
        code = 8 * signs[a]
        for j in range(1, 8):
            code = code + jnp.where(jnp.broadcast_to(dest[j : j + 1, :], (8, LANES)) == row, j, 0)
        code_t[8 * a : 8 * a + 8, :] = code
    wait(move)
    keep = fetch([(dest_t, dest_hbm)], sem)

    bounds = [0, THIRD, 2 * THIRD, 3 * THIRD, PAD]
    out_up = [pltpu.make_async_copy(buf_p.at[a:b], up_hbm.at[a:b], out_sem.at[k]) for k, (a, b) in enumerate(zip(bounds, bounds[1:]))]
    out_early = pltpu.make_async_copy(buf_n.at[PAD - EARLY : PAD], early_hbm, out_sem.at[4])
    out_late = pltpu.make_async_copy(buf_n.at[0 : PAD - EARLY], late_hbm, out_sem.at[5])

    def step(c, carry):
        piece(c).wait()
        codes = pltpu.roll(code_t[...], LANES - STEP * c, 1)
        for i in range(STEP):
            r = STEP * c + i
            for a in range(16):
                at = 256 * r + 16 * a
                first = f_ref[pl.ds(at, 8, stride=2), :]
                last = f_ref[pl.ds(at + 1, 8, stride=2), :]
                code = spread(codes[8 * a : 8 * a + 8, :], i)
                sent = jnp.where(code >= 8, last, first)
                sent = jnp.take_along_axis(sent, code & 7, axis=0)
                buf_p[pl.ds(table_s[a, r], 8), :] = sent
                buf_n[pl.ds(table_s[16 + a, r], 8), :] = sent
        now, then = table_s[0, STEP * c + STEP], table_s[0, STEP * c]
        for k in range(3):
            @pl.when((now >= THIRD * (k + 1)) & (then < THIRD * (k + 1)))
            def _():
                out_up[k].start()

        now, then = table_s[16, STEP * c + STEP], table_s[16, STEP * c]

        @pl.when((now <= HALF - EARLY) & (then > HALF - EARLY))
        def _():
            out_early.start()

        return carry

    lax.fori_loop(0, CHUNKS, step, 0)
    out_up[3].start()
    out_late.start()
    wait([*out_up, out_early, out_late])
    wait(keep)


def shift_lanes(x, by):
    lane = iota(x.shape, 1)
    if by > 0:
        return jnp.where(lane == 0, 0.0, pltpu.roll(x, 1, 1))
    return jnp.where(lane == LANES - 1, 0.0, pltpu.roll(x, LANES - 1, 1))


def dot(a, b):
    return jnp.dot(a, b, precision=HIGHEST, preferred_element_type=F32)


def sums_kernel(f_hbm, v_hbm, tau_hbm, side_ref, other_ref, wall_hbm, heat_hbm, c_hbm, out_hbm,
                f_ref, v_ref, tau_ref, wall_ref, heat_ref, c_ref, out_ref, sem, f_sem):
    read_v = fetch([(v_hbm, v_ref)], sem)
    piece = pieces(f_hbm, f_ref, f_sem, 2 * LANES)
    for c in range(CHUNKS):
        piece(c).start()
    wait(read_v)
    others = fetch([(tau_hbm, tau_ref), (wall_hbm, wall_ref), (heat_hbm, heat_ref), (c_hbm, c_ref)], sem)
    weight = SPACING**3
    classes = iota((VGRID, LANES), 0).astype(F32)

    def step(c, sums):
        piece(c).wait()
        for i in range(STEP):
            r = STEP * c + i
            sx, sy, sz, sq, n = fields(v_ref[pl.ds(r, 1), :])
            row_4 = (2.0 / 3.0 * sq - 1.0) * weight
            heat = (sq - 2.5) * weight
            moments = jnp.concatenate(
                [jnp.full_like(sx, weight), sx * weight, sy * weight, sz * weight, row_4, sx * heat, sy * heat, sz * heat], 0
            )
            hot = classes == n
            parts = [moments]
            for speed in (sx, sy):
                along = row_4 * jnp.abs(speed)
                parts.append(jnp.where(hot, jnp.where(speed > 0, along, 0.0), 0.0))
                parts.append(jnp.where(hot, jnp.where(speed > 0, 0.0, along), 0.0))
            high, low = split(jnp.concatenate(parts, 0))
            both = jnp.concatenate([f_ref[pl.ds(256 * r + x, LANES, stride=2), :] for x in range(2)], 1)
            f_high, f_low = split(both)
            sums = sums + jnp.dot(
                jnp.concatenate([high, high, low], 1), jnp.concatenate([f_high, f_low, f_high], 0),
                preferred_element_type=F32,
            )
        return sums

    sums = lax.fori_loop(0, CHUNKS, step, jnp.zeros((8 + 4 * VGRID, 2 * LANES), F32))
    wait(others)

    def part(x, k):
        return sums[8 + VGRID * k : 8 + VGRID * (k + 1), LANES * x : LANES * (x + 1)]

    def inverse(tau):
        return 1.0 / (1.0 / tau + classes * SPACING)

    where_vel = 2 * lax.axis_index("chip") + lax.axis_index("core")
    lead = jnp.where(where_vel == 0, 1.0, 0.0)
    core = lax.rem(where_vel, 2)
    before = jnp.where(core == 0, side_ref[1:2, :], other_ref[1:2, :])
    after = jnp.where(core == 0, other_ref[0:1, :], side_ref[0:1, :])
    rows = []
    for x in range(2):
        tau = tau_ref[x : x + 1, :]
        inv = inverse(tau)
        kernels = dot(c_ref[...], inv) * (1.0 / tau)
        moments = sums[0:8, LANES * x : LANES * (x + 1)]
        product = moments * kernels
        gas = jnp.sum(product, 0, keepdims=True)
        wall = product[0:1, :] + lead * heat_ref[x : x + 1, :] * kernels[4:5, :]
        held = jnp.where(wall_ref[x : x + 1, :] == 1, wall, gas) - moments[4:5, :]
        across = part(1, 1) if x == 0 else part(0, 0)
        moved = inv * (across + shift_lanes(part(x, 2), 1) + shift_lanes(part(x, 3), -1))
        out_ref[8 * x : 8 * x + 8, :] = moments
        rows.append(held + jnp.sum(moved, 0, keepdims=True))
    rows.append(jnp.sum(inverse(before) * part(0, 1), 0, keepdims=True))
    rows.append(jnp.sum(inverse(after) * part(1, 0), 0, keepdims=True))
    for j in range(4):
        out_ref[16 + j : 17 + j, :] = rows[j]
    out_ref[20:24, :] = jnp.zeros((4, LANES), F32)
    wait(fetch([(out_ref, out_hbm)], sem))


def merge_kernel(mine_hbm, other_hbm, tau_hbm, payload_hbm, moments_hbm, mine_ref, other_ref, tau_ref, moments_ref, payload, sem):
    wait(fetch([(mine_hbm, mine_ref), (other_hbm, other_ref), (tau_hbm, tau_ref)], sem))
    both = mine_ref[...] + other_ref[...]
    moments_ref[...] = both[0:16, :]
    for k in range(4):
        payload[ROWS * k : ROWS * k + 4, :] = both[16:20, :]
        payload[ROWS * k + 4 : ROWS * k + 6, :] = tau_ref[...]
    block = payload[0 : 4 * ROWS, :]
    for k in range(1, payload.shape[0] // (4 * ROWS)):
        payload[4 * ROWS * k : 4 * ROWS * (k + 1), :] = block
    wait(fetch([(moments_ref, moments_hbm), (payload, payload_hbm)], sem))


def sweep_kernel(f_hbm, v_hbm, mine_hbm, other_hbm, tau_hbm, wall_hbm, heat_hbm, pre_hbm, along_hbm, shape_hbm,
                 f_ref, v_ref, mine_ref, other_ref, tau_ref, wall_ref, heat_ref, pre_ref, along_ref, shape_ref,
                 rhs, cols, sem, f_sem, pre_sem, along_sem):
    first = fetch([(v_hbm, v_ref), (mine_hbm, mine_ref), (other_hbm, other_ref), (tau_hbm, tau_ref), (wall_hbm, wall_ref),
                   (heat_hbm, heat_ref)], sem)
    piece = pieces(f_hbm, f_ref, f_sem, 2 * LANES)
    for c in range(CHUNKS):
        piece(c).start()
    outs = [pieces(pre_ref, pre_hbm, pre_sem, 2 * LANES), pieces(along_ref, along_hbm, along_sem, LANES)]
    rhs[...] = jnp.zeros((LANES, 6 * LANES), F32)
    shape_ref[...] = jnp.zeros((LANES, LANES), F32)
    cols[...] = jnp.zeros((LANES, LANES), F32)
    row = iota((8, LANES), 0)
    classes = iota((VGRID, LANES), 0).astype(F32)
    wait(first)
    for x in range(2):
        part = slice(8 * x, 8 * x + 8)
        moments = mine_ref[part, :] + other_ref[part, :]
        wall = jnp.where(row == 0, moments, jnp.where(row == 4, heat_ref[x : x + 1, :], 0.0))
        relax = 1.0 / tau_ref[x : x + 1, :]
        adjusted = jnp.where(wall_ref[x : x + 1, :] == 1, wall, moments)
        high, low = (p.astype(F32) for p in split(adjusted * relax))
        here = slice(LANES * x, LANES * (x + 1))
        rhs[0:8, here] = high
        rhs[8:16, here] = low
        rhs[16:24, here] = high
        high, low = (p.astype(F32) for p in split(1.0 / (relax + classes * SPACING)))
        here = slice(LANES * (2 + x), LANES * (3 + x))
        rhs[24:48, here] = high
        rhs[48:72, here] = low
    for k in range(2):
        rhs[72:80, LANES * (4 + k) : LANES * (5 + k)] = jnp.where(row == k, 1.0, 0.0)
    rhs_value = rhs[...].astype(BF16)

    def step(c, carry):
        piece(c).wait()
        for i in range(STEP):
            r = STEP * c + i
            sx, sy, sz, sq, n = fields(v_ref[pl.ds(r, 1), :])
            maxwell = jnp.exp(-sq) * math.pi**-1.5
            shape = (sq - 1.5) * maxwell
            heat = SHAKHOV * (sq - 2.5) * maxwell
            high, low = (p.astype(F32) for p in split(jnp.concatenate(
                [maxwell, 2.0 * sx * maxwell, 2.0 * sy * maxwell, 2.0 * sz * maxwell,
                 (1.0 - COOLING) * shape, sx * heat, sy * heat, sz * heat], 0)))
            shape_ref[pl.ds(r, 1), :] = shape
            hot = jnp.where(classes == n, 1.0, 0.0)
            zero = jnp.zeros_like(sx)
            cols[0:80, :] = jnp.concatenate(
                [high, high, low, hot, hot, sx, sy, zero, zero, zero, zero, zero, zero], 0)
            made = jnp.dot(cols[...].T.astype(BF16), rhs_value, preferred_element_type=F32)
            speed_x, speed_y = made[:, 4 * LANES : 5 * LANES], made[:, 5 * LANES : 6 * LANES]
            rows = [f_ref[pl.ds(256 * r + x, LANES, stride=2), :] for x in range(2)]
            along_x, along_y = jnp.abs(speed_x), jnp.abs(speed_y)
            ahead = speed_x > 0
            for x in range(2):
                upwind_y = jnp.where(speed_y > 0, shift_lanes(rows[x], 1), shift_lanes(rows[x], -1))
                near = jnp.where(ahead, 0.0, rows[1]) if x == 0 else jnp.where(ahead, rows[0], 0.0)
                inv = made[:, LANES * (2 + x) : LANES * (3 + x)]
                value = (made[:, LANES * x : LANES * (x + 1)] + along_x * near + along_y * upwind_y) * inv
                pre_ref[pl.ds(256 * r + x, LANES, stride=2), :] = value
            at = pl.ds(pl.multiple_of(LANES * r, LANES), LANES)
            along_ref[at, :] = speed_x * jnp.where(ahead, made[:, 2 * LANES : 3 * LANES], made[:, 3 * LANES : 4 * LANES])
        for out in outs:
            out(c).start()
        return carry

    lax.fori_loop(0, CHUNKS, step, 0)
    shape_ref[...] = shape_ref[...].T
    keep = fetch([(shape_ref, shape_hbm)], sem)
    wait(keep)
    for c in range(CHUNKS):
        for out in outs:
            out(c).wait()


def finish_kernel(pre_hbm, along_hbm, shape_hbm, dest_hbm, table_hbm, y_hbm, up_hbm, early_hbm, late_hbm, out_hbm, corr_ref,
                  pre_ref, along_ref, shape_t, dest_t, table_s, y_ref, buf_p, buf_n, kept, out_ref, sem, pre_sem, along_sem, out_sem):
    copies = fetch([(y_hbm, y_ref), (table_hbm, table_s), (shape_hbm, shape_t), (dest_hbm, dest_t), (up_hbm, buf_p),
                    (early_hbm, buf_n.at[PAD - EARLY : PAD]), (late_hbm, buf_n.at[0 : PAD - EARLY])], sem)
    ins = [pieces(pre_hbm, pre_ref, pre_sem, 2 * LANES), pieces(along_hbm, along_ref, along_sem, LANES)]
    done = pieces(out_ref, out_hbm, out_sem, 2 * LANES)
    for c in range(CHUNKS):
        for piece in ins:
            piece(c).start()
    copies[0].wait()

    def take(device, j):
        return y_ref[pl.ds(ROWS * device + j, 64, stride=ROWS), :]

    place = iota((64, LANES), 0)

    def lower(x):
        return jnp.where(place == 0, 0.0, pltpu.roll(x, 1, 0))

    def upper(x):
        return jnp.where(place == 63, 0.0, pltpu.roll(x, 63, 0))

    def over_vel(j):
        return take(0, j) + take(64, j)

    even = over_vel(0) + lower(over_vel(3))
    odd = over_vel(1) + upper(over_vel(2))
    middle_even = COOLING / take(0, 4) + 4.0
    middle_odd = COOLING / take(0, 5) + 4.0

    def operate(e, o):
        image_e = middle_even * e - (lower(o) + o + shift_lanes(e, 1) + shift_lanes(e, -1))
        image_o = middle_odd * o - (e + upper(e) + shift_lanes(o, 1) + shift_lanes(o, -1))
        return image_e, image_o

    def inner(a, b):
        total = jnp.sum(a[0] * b[0] + a[1] * b[1], 0, keepdims=True)
        return jnp.sum(total, 1, keepdims=True)

    residual = (even, odd)
    direction = residual
    found = (jnp.zeros_like(even), jnp.zeros_like(odd))
    norm_now = inner(residual, residual)
    for rounds in range(ITERS):
        image = operate(*direction)
        step_size = norm_now / inner(direction, image)
        found = tuple(v + step_size * d for v, d in zip(found, direction))
        if rounds + 1 < ITERS:
            residual = tuple(r - step_size * i for r, i in zip(residual, image))
            norm_next = inner(residual, residual)
            direction = tuple(r + norm_next / norm_now * d for r, d in zip(residual, direction))
            norm_now = norm_next
    kept[0:64, :] = found[0]
    kept[64:128, :] = found[1]
    where_space = lax.axis_index("space")
    corr_ref[0:1, :] = kept[pl.ds(where_space, 1), :]
    corr_ref[1:2, :] = kept[pl.ds(64 + where_space, 1), :]
    wait(copies[1:])
    corr = [jnp.broadcast_to(corr_ref[x : x + 1, :], (8, LANES)) for x in range(2)]
    row = iota((8, LANES), 0)

    def step(c, carry):
        for piece in ins:
            piece(c).wait()
        shapes = pltpu.roll(shape_t[...], LANES - STEP * c, 1)
        dests = pltpu.roll(dest_t[...], LANES - STEP * c, 1)
        for i in range(STEP):
            r = STEP * c + i
            for a in range(16):
                at = 128 * r + 8 * a
                here = pl.ds(pl.multiple_of(at, 8), 8)
                halo = jnp.where(row < table_s[32 + a, r], buf_p[pl.ds(table_s[a, r], 8), :],
                                 buf_n[pl.ds(table_s[16 + a, r], 8), :])
                along = along_ref[here, :]
                moved = along * jnp.take_along_axis(halo, spread(dests[8 * a : 8 * a + 8, :], i), axis=0)
                ahead = along > 0
                shape = spread(shapes[8 * a : 8 * a + 8, :], i)
                near = pl.ds(2 * at, 8, stride=2)
                far = pl.ds(2 * at + 1, 8, stride=2)
                out_ref[near, :] = pre_ref[near, :] + jnp.where(ahead, moved, 0.0) + shape * corr[0]
                out_ref[far, :] = pre_ref[far, :] - jnp.where(ahead, 0.0, moved) + shape * corr[1]
        done(c).start()
        return carry

    lax.fori_loop(0, CHUNKS, step, 0)
    for c in range(CHUNKS):
        done(c).wait()


def vmem(shape, dtype=F32):
    return pltpu.VMEM(shape, dtype)


def struct(shape, dtype=F32):
    return jax.ShapeDtypeStruct(shape, dtype)


IN_HBM = pl.BlockSpec(memory_space=pltpu.HBM)
IN_VMEM = pl.BlockSpec(memory_space=pltpu.VMEM)
DMA = pltpu.SemaphoreType.DMA
INT = jnp.int32


def call(kernel, outs, scratch, args, flops, out_specs=None, local=(), alias=None):
    return pl.pallas_call(
        kernel,
        out_shape=outs,
        in_specs=[IN_VMEM if i in local else IN_HBM for i in range(len(args))],
        out_specs=jax.tree.map(lambda _: IN_HBM, outs) if out_specs is None else out_specs,
        scratch_shapes=scratch,
        input_output_aliases=alias or {},
        compiler_params=pltpu.CompilerParams(vmem_limit_bytes=52 << 20),
        cost_estimate=pl.CostEstimate(flops=flops, bytes_accessed=8 << 20, transcendentals=0),
    )(*args)


def program(distribution, vel_index, collision_time, wall_flags, wall_temp):
    space = lax.axis_size("space")
    chips = lax.axis_size("chip")
    up = [(i, i + 1) for i in range(space - 1)]
    down = [(j, i) for i, j in up]
    both = []
    for v in range(2 * chips):
        both += [(v * space + i, v * space + j) for i, j in (up if v % 2 == 0 else down)]

    swap = [(0, 1), (1, 0)]
    ring = []
    for c in range(chips):
        for k in range(space):
            ring.append((c * space + k, c * space + k + 1 if k % 2 == 0 else (c + 1) % chips * space + k - 1))
    flat = distribution.reshape(2 * SLOTS, LANES)
    ids = vel_index.reshape(BLOCKS, LANES)
    small, square, whole, halves = (2, LANES), (LANES, LANES), (2 * SLOTS, LANES), (SLOTS, LANES)
    side = lax.ppermute(collision_time, ("chip", "core", "space"), both)
    rows_up, rows_early, rows_late, dest, table = call(
        compact_kernel,
        (struct((PAD, LANES)), struct((EARLY, LANES)), struct((PAD - EARLY, LANES)), struct(square, INT), struct((48, LANES), INT)),
        [vmem(whole), vmem((BLOCKS, LANES), INT), vmem(square), vmem(square, INT), vmem(square, INT), vmem((48, LANES), INT),
         vmem((PAD, LANES)), vmem((PAD, LANES)), pltpu.SMEM((48, LANES), INT), DMA((2,)), DMA((CHUNKS,)), DMA((6,))],
        (flat, ids), 1 << 20,
    )
    halo_up = lax.ppermute(rows_up, "space", up)
    halo_early = lax.ppermute(rows_early, "space", down)
    side_other = lax.ppermute(side, "core", swap)
    sums = call(
        sums_kernel, struct((24, LANES)),
        [vmem(whole), vmem((BLOCKS, LANES), INT), vmem(small), vmem(small, INT), vmem(small),
         vmem((8, VGRID)), vmem((24, LANES)), DMA((4,)), DMA((CHUNKS,))],
        (flat, ids, collision_time, side, side_other, wall_flags, wall_temp, jnp.asarray(class_constants())), 1 << 30,
        local=(3, 4),
    )
    sums_other = lax.ppermute(sums, "core", swap)
    gather = ROWS * chips * space
    payload, moments = call(
        merge_kernel, (struct((gather, LANES)), struct((16, LANES))),
        [vmem((24, LANES)), vmem((24, LANES)), vmem(small), vmem((16, LANES)), vmem((gather, LANES)), DMA((3,))],
        (sums, sums_other, collision_time), 1 << 16,
    )
    gathered = lax.all_to_all(payload.reshape(chips * space, 1, ROWS * LANES), ("chip", "space"), 0, 0, tiled=True)
    moments_other = lax.ppermute(lax.ppermute(moments, ("chip", "space"), ring), ("chip", "space"), ring)
    halo_late = lax.ppermute(rows_late, "space", down)
    pre, along, shape = call(
        sweep_kernel,
        (struct(whole), struct(halves), struct(square)),
        [vmem(whole), vmem((BLOCKS, LANES), INT), vmem((16, LANES)), vmem((16, LANES)), vmem(small), vmem(small, INT), vmem(small),
         vmem(whole), vmem(halves), vmem(square), vmem((LANES, 6 * LANES)), vmem(square),
         DMA((6,)), DMA((CHUNKS,)), DMA((CHUNKS,)), DMA((CHUNKS,))],
        (flat, ids, moments, moments_other, collision_time, wall_flags, wall_temp), 1 << 30,
    )
    result, correction = call(
        finish_kernel, (struct(whole), struct(small)),
        [vmem(whole), vmem(halves), vmem(square), vmem(square, INT), pltpu.SMEM((48, LANES), INT), vmem((gather, LANES)),
         vmem((PAD, LANES)), vmem((PAD, LANES)), vmem(square), vmem(whole), DMA((7,))] + [DMA((CHUNKS,))] * 3,
        (pre, along, shape, dest, table, gathered.reshape(gather, LANES), halo_up, halo_early, halo_late), 1 << 24,
        (IN_HBM, IN_VMEM),
    )
    return result.reshape(SLOTS, 2, LANES), correction


def solution(mesh):
    vel, space = mesh.devices.shape
    mesh = jax.sharding.Mesh(mesh.devices.reshape(vel // 2, 2, space), ("chip", "core", "space"))
    cores = ("chip", "core")
    placed = (P(cores, "space", None), P(cores), P("space", None), P("space", None), P("space", None))
    return jax.shard_map(
        program,
        mesh=mesh,
        in_specs=placed,
        out_specs=(P(cores, "space", None), P("space", None)),
        check_vma=False,
    )
```
